32 devices in a mesh: lat: 4 (over z), lon: 8 (over y, x, core).
Axes of the slice: x: 2, y: 2, z: 4, core: 2. Of those that a mesh axis runs over, the one named last changes fastest.
Arguments:
- atmos_state: bfloat16 [128, 512, 256], P('lat', 'lon'), may hold values from -6 to 6
- ocean_state: bfloat16 [192, 512, 128], P('lat', 'lon'), may hold values from -6 to 6
- atmos_cotangent: bfloat16 [128, 512, 256], P('lat', 'lon'), may hold values from -0.011962891 to 0.011962891
- ocean_cotangent: bfloat16 [192, 512, 128], P('lat', 'lon'), may hold values from -0.011962891 to 0.011962891
- land_sea: int32 [192, 512], P('lat', 'lon'), may hold values 0 or 1
- fold_partner: int32 [512], replicated, may hold values from 0 to 511, as said below
- ocean_pairs: int32 [96, 8, 4], P('lat', 'lon'), may hold values from 0 to 511, as said below
- ocean_counts: int32 [96, 8], P('lat', 'lon'), may hold values from 1 to 4
- ocean_weights: bfloat16 [96, 8, 4, 128, 128], P('lat', 'lon'), may hold values from -0.25 to 0.25
- atmos_pairs: int32 [64, 8, 4], P('lat', 'lon'), may hold values from 0 to 767, as said below
- atmos_counts: int32 [64, 8], P('lat', 'lon'), may hold values from 1 to 4
- atmos_weights: bfloat16 [64, 8, 4, 128, 128], P('lat', 'lon'), may hold values from -0.25 to 0.25
- flux_map: bfloat16 [256, 16], replicated, may hold values from -0.375 to 0.375
- surface_map: bfloat16 [128, 16], replicated, may hold values from -0.5 to 0.5
- flux_inject: bfloat16 [16, 128], replicated, may hold values from -1.5 to 1.5
- surface_inject: bfloat16 [16, 256], replicated, may hold values from -1.5 to 1.5
- atmos_kernel: bfloat16 [49, 256], replicated, may hold values from -0.875 to 0.875
- atmos_gain: bfloat16 [256], replicated, may hold values from 0.25 to 1.75
- atmos_w_in: bfloat16 [256, 1024], replicated, may hold values from -0.375 to 0.375
- atmos_w_out: bfloat16 [1024, 256], replicated, may hold values from -0.1875 to 0.1875
- ocean_kernel: bfloat16 [49, 128], replicated, may hold values from -0.875 to 0.875
- ocean_gain: bfloat16 [128], replicated, may hold values from 0.25 to 1.75
- ocean_w_in: bfloat16 [128, 512], replicated, may hold values from -0.5 to 0.5
- ocean_w_out: bfloat16 [512, 128], replicated, may hold values from -0.25 to 0.25
Outputs:
- atmos_next: bfloat16 [128, 512, 256], P('lat', 'lon')
- ocean_next: bfloat16 [192, 512, 128], P('lat', 'lon')
- atmos_kernel_grad: float32 [49, 256], replicated
- atmos_gain_grad: float32 [256], replicated
- atmos_w_in_grad: float32 [256, 1024], replicated
- atmos_w_out_grad: float32 [1024, 256], replicated
- ocean_kernel_grad: float32 [49, 128], replicated
- ocean_gain_grad: float32 [128], replicated
- ocean_w_in_grad: float32 [128, 512], replicated
- ocean_w_out_grad: float32 [512, 128], replicated
The draws below stay inside these ranges and needn't reach their ends.
Inputs may be any that keep to these rules, and one draw needn't show every extreme that they name: `ocean_pairs`: each entry is (owner device) * 16 + (block index on that device), devices numbered lat-major; the owner lies in the same latitude band as the ocean block or an adjacent one, and in the same longitude sector or an adjacent one, sectors wrapping around. `atmos_pairs`: each entry is (owner device) * 24 + (block index on that device), devices numbered lat-major; the owner lies in the same latitude band as the atmosphere block or an adjacent one, and in the same longitude sector or an adjacent one, sectors wrapping around. `ocean_counts`: only the first count entries of a block's list are live. `atmos_counts`: only the first count entries of a block's list are live. `fold_partner`: an involution: the partner of a column's partner is the column. `land_sea`: 1 on ocean cells, 0 on land.
All inputs are finite; a program needn't handle non-finite values. No bound on the sum of `land_sea` on one device may be relied on, other than what follows from the above.
Results may differ from the reference program's by a relative error of at most 0.0075.
Values may be sent and summed in bfloat16 or wider, within the bound.
A program may use at most 128 MiB of HBM per device.

```python
from functools import partial
import jax
import jax.numpy as jnp
from jax import lax

CA = 256
CO = 128
HA = 1024
HO = 512
NFIELD = 16
BCELLS = 128
PAIRS = 4
COLS = 64
AR = 32
OR = 48
BROWS = 2
ABLK = 16
OBLK = 24
LAT_BANDS = 4
LON_SECTORS = 8
ALAT = 128
OLAT = 192
LON_CELLS = 512


def owner_entries(key_device, device_number, entries, source_blocks):
    key_lat, key_lon, key_local = jax.random.split(key_device, 3)
    band = device_number // LON_SECTORS
    sector = device_number % LON_SECTORS
    lat_step = jax.random.randint(key_lat, (entries,), -1, 2)
    lon_step = jax.random.randint(key_lon, (entries,), -1, 2)
    owner_band = jnp.clip(band + lat_step, 0, LAT_BANDS - 1)
    owner_sector = (sector + lon_step) % LON_SECTORS
    owners = (owner_band * LON_SECTORS + owner_sector).astype(jnp.int32)
    local_ids = jax.random.randint(key_local, (entries,), 0, source_blocks)
    return owners * source_blocks + local_ids


def pair_listing(key, salt, block_count, source_blocks):
    device_total = LAT_BANDS * LON_SECTORS
    device_keys = jax.random.split(jax.random.fold_in(key, salt), device_total)
    maker = partial(owner_entries, entries=block_count * PAIRS, source_blocks=source_blocks)
    listing = jax.vmap(maker)(device_keys, jnp.arange(device_total, dtype=jnp.int32))
    listing = listing.reshape(LAT_BANDS, LON_SECTORS, block_count, PAIRS).transpose(0, 2, 1, 3)
    return listing.reshape(LAT_BANDS * block_count, LON_SECTORS, PAIRS).astype(jnp.int32)


def draw_ocean_pairs(key, part):
    return pair_listing(key, 11, OBLK, ABLK)


def draw_atmos_pairs(key, part):
    return pair_listing(key, 23, ABLK, OBLK)


def draw_fold_partner(key, part):
    pole_column = jax.random.randint(jax.random.fold_in(key, 5), (), 0, LON_CELLS)
    return ((pole_column - 1 - jnp.arange(LON_CELLS, dtype=jnp.int32)) % LON_CELLS).astype(jnp.int32)


def set_ends(drawn, key, least, largest):
    longest = drawn.shape.index(max(drawn.shape))
    spots = []
    for shift in (0, 1):
        where = [jax.random.randint(jax.random.fold_in(key, axis), (), 0, length) for axis, length in enumerate(drawn.shape)]
        where[longest] = (where[longest] + shift) % drawn.shape[longest]
        spots.append(tuple(where))
    return drawn.at[spots[0]].set(least).at[spots[1]].set(largest)


def block_levels(stream_key, dims, pieces, smallest, largest):
    level, own = 1.0, jax.random.fold_in(stream_key, 6)
    for dim, blocks in pieces:
        heights = jnp.exp(jax.random.uniform(jax.random.fold_in(own, dim), (blocks,), jnp.float32, smallest / len(pieces), largest / len(pieces)))
        level = level * jnp.repeat(heights, dims[dim] // blocks).reshape([-1 if axis == dim else 1 for axis in range(len(dims))])
    return level


def noise(stream_key, extent, spread, most, cuts=(), held_as=jnp.bfloat16):
    values = jax.random.normal(stream_key, extent, jnp.float32) * spread
    if len(cuts) > 0:
        values = block_levels(stream_key, extent, cuts, -0.22, 0.18) * values
    return jnp.clip(values, min=-most, max=most).astype(held_as)


def setup_inputs(seed: int = 0) -> dict:
    keys = jax.random.split(jax.random.key(seed), 25)
    return {
        "atmos_state": noise(keys[0], (ALAT, LON_CELLS, CA), 1.0, 6.0, ((0, 4), (1, 8))),
        "ocean_state": noise(keys[1], (OLAT, LON_CELLS, CO), 1.0, 6.0, ((0, 4), (1, 8))),
        "atmos_cotangent": noise(keys[2], (ALAT, LON_CELLS, CA), 0.002, 0.011962891, ((0, 4), (1, 8))),
        "ocean_cotangent": noise(keys[3], (OLAT, LON_CELLS, CO), 0.002, 0.011962891, ((0, 4), (1, 8))),
        "land_sea": set_ends((jax.random.randint(keys[4], (OLAT, LON_CELLS), 0, 10) < 7).astype(jnp.int32), jax.random.fold_in(keys[4], 1), 0, 1),
        "fold_partner": draw_fold_partner(jax.random.fold_in(keys[24], 71), 0),
        "ocean_pairs": draw_ocean_pairs(jax.random.fold_in(keys[24], 71), 0),
        "ocean_counts": set_ends(jax.random.randint(keys[7], (OLAT // BROWS, LON_SECTORS), 1, PAIRS + 1), jax.random.fold_in(keys[7], 1), 1, PAIRS).astype(jnp.int32),
        "ocean_weights": noise(keys[8], (OLAT // BROWS, LON_SECTORS, PAIRS, BCELLS, BCELLS), (PAIRS * BCELLS) ** -0.5, 0.25, ((0, 4), (1, 8))),
        "atmos_pairs": draw_atmos_pairs(jax.random.fold_in(keys[24], 71), 0),
        "atmos_counts": set_ends(jax.random.randint(keys[10], (ALAT // BROWS, LON_SECTORS), 1, PAIRS + 1), jax.random.fold_in(keys[10], 1), 1, PAIRS).astype(jnp.int32),
        "atmos_weights": noise(keys[11], (ALAT // BROWS, LON_SECTORS, PAIRS, BCELLS, BCELLS), (PAIRS * BCELLS) ** -0.5, 0.25, ((0, 4), (1, 8))),
        "flux_map": noise(keys[12], (CA, NFIELD), CA ** -0.5, 0.375),
        "surface_map": noise(keys[13], (CO, NFIELD), CO ** -0.5, 0.5),
        "flux_inject": noise(keys[14], (NFIELD, CO), NFIELD ** -0.5, 1.5),
        "surface_inject": noise(keys[15], (NFIELD, CA), NFIELD ** -0.5, 1.5),
        "atmos_kernel": noise(keys[16], (49, CA), 49 ** -0.5, 0.875),
        "atmos_gain": jnp.clip(1.0 + 0.15 * jax.random.normal(keys[17], (CA,), jnp.float32), 0.25, 1.75).astype(jnp.bfloat16),
        "atmos_w_in": noise(keys[18], (CA, HA), CA ** -0.5, 0.375),
        "atmos_w_out": noise(keys[19], (HA, CA), HA ** -0.5, 0.1875),
        "ocean_kernel": noise(keys[20], (49, CO), 49 ** -0.5, 0.875),
        "ocean_gain": jnp.clip(1.0 + 0.15 * jax.random.normal(keys[21], (CO,), jnp.float32), 0.25, 1.75).astype(jnp.bfloat16),
        "ocean_w_in": noise(keys[22], (CO, HO), CO ** -0.5, 0.5),
        "ocean_w_out": noise(keys[23], (HO, CO), HO ** -0.5, 0.25),
    }


epsilon = 1e-06

def contract_rows(left, right):
    return lax.dot_general(left, right, (((0,), (0,)), ((), ())), preferred_element_type=jnp.float32)

def block_pass(padded, cotangent, keep_mask, kernel, gain, w_in, w_out):
    row_count = padded.shape[0] - 6
    col_count = padded.shape[1] - 6
    channels = padded.shape[2]
    convolved = jnp.zeros((row_count, col_count, channels), jnp.float32)
    for offset in range(49):
        tap_row = offset // 7
        tap_col = offset % 7
        window = padded[tap_row:tap_row + row_count, tap_col:tap_col + col_count, :].astype(jnp.float32)
        convolved = convolved + window * kernel[offset].astype(jnp.float32)
    centre = convolved - lax.optimization_barrier(jnp.mean(convolved, axis=-1, keepdims=True))
    inv_spread = lax.rsqrt(lax.optimization_barrier(jnp.mean(centre * centre, axis=-1, keepdims=True)) + epsilon)
    unit_part = centre * inv_spread
    gain_wide = gain.astype(jnp.float32)
    normed = (unit_part * gain_wide).astype(jnp.bfloat16).reshape(row_count * col_count, channels)
    pre_act = jnp.dot(normed, w_in, preferred_element_type=jnp.float32)
    hidden = jax.nn.gelu(pre_act).astype(jnp.bfloat16)
    update = jnp.dot(hidden, w_out, preferred_element_type=jnp.float32).reshape(row_count, col_count, channels)
    interior = padded[3:3 + row_count, 3:3 + col_count, :].astype(jnp.float32)
    result = ((interior + update) * keep_mask).astype(jnp.bfloat16)
    upstream = (cotangent.astype(jnp.float32) * keep_mask).astype(jnp.bfloat16).reshape(row_count * col_count, channels)
    grad_out = contract_rows(hidden, upstream)
    grad_hidden = lax.dot_general(upstream, w_out, (((1,), (1,)), ((), ())), preferred_element_type=jnp.float32)
    _, gelu_back = jax.vjp(jax.nn.gelu, pre_act)
    grad_pre = gelu_back(grad_hidden)[0].astype(jnp.bfloat16)
    grad_in = contract_rows(normed, grad_pre)
    grad_normed = lax.dot_general(grad_pre, w_in, (((1,), (1,)), ((), ())), preferred_element_type=jnp.float32)
    grad_normed = grad_normed.reshape(row_count, col_count, channels)
    grad_gain = lax.optimization_barrier(jnp.sum(grad_normed * unit_part, axis=(0, 1)))
    grad_unit = grad_normed * gain_wide
    grad_conv = inv_spread * (grad_unit - lax.optimization_barrier(jnp.mean(grad_unit, axis=-1, keepdims=True)) - unit_part * lax.optimization_barrier(jnp.mean(grad_unit * unit_part, axis=-1, keepdims=True)))
    tap_sums = []
    for offset in range(49):
        tap_row = offset // 7
        tap_col = offset % 7
        window = padded[tap_row:tap_row + row_count, tap_col:tap_col + col_count, :].astype(jnp.float32)
        tap_sums.append(lax.optimization_barrier(jnp.sum(grad_conv * window, axis=(0, 1))))
    grad_kernel = jnp.stack(tap_sums)
    return (result, (grad_kernel, grad_gain, grad_in, grad_out))

def make_blocks(source, projection, keep_cells, block_count):
    channels = source.shape[2]
    shaped = source.reshape(LAT_BANDS, block_count, BROWS, LON_SECTORS, COLS, channels)
    shaped = shaped.transpose(0, 3, 1, 2, 4, 5).reshape(-1, BCELLS, channels)
    kept = keep_cells.reshape(LAT_BANDS, block_count, BROWS, LON_SECTORS, COLS)
    kept = kept.transpose(0, 3, 1, 2, 4).reshape(-1, 1, BCELLS)
    values = jnp.einsum('nkc,cf->nfk', shaped.astype(jnp.float32), projection.astype(jnp.float32), precision=lax.Precision.HIGHEST)
    return (values * kept).astype(jnp.bfloat16)

def remap(listing, pairs, counts, weights):

    def one_row(items):
        row_pairs, row_counts, row_weights = items
        picked = jnp.take(listing, row_pairs, axis=0).astype(jnp.float32)
        in_use = (jnp.arange(PAIRS)[None, :] < row_counts[:, None]).astype(jnp.float32)
        picked = picked * in_use[:, :, None, None]
        return jnp.einsum('spfc,spcd->sfd', picked, row_weights.astype(jnp.float32), precision=lax.Precision.HIGHEST)
    return lax.map(one_row, (pairs, counts, weights)).astype(jnp.bfloat16)

def inject(state, remapped, block_count, projection):
    grid_rows = remapped.reshape(LAT_BANDS * block_count, LON_SECTORS, NFIELD, BROWS, COLS)
    grid_rows = grid_rows.transpose(0, 3, 1, 4, 2).reshape(LAT_BANDS * block_count * BROWS, LON_CELLS, NFIELD)
    added = jnp.einsum('ijf,fc->ijc', grid_rows.astype(jnp.float32), projection.astype(jnp.float32), precision=lax.Precision.HIGHEST)
    return (state.astype(jnp.float32) + added).astype(jnp.bfloat16)

def run_grid(padded, cotangent, keep_mask, kernel, gain, w_in, w_out, band_rows):
    channels = padded.shape[2]
    hidden_width = w_in.shape[1]
    initial = (jnp.zeros((49, channels), jnp.float32), jnp.zeros((channels,), jnp.float32), jnp.zeros((channels, hidden_width), jnp.float32), jnp.zeros((hidden_width, channels), jnp.float32))

    def one_band(totals, band_index):
        low_row = (band_index * band_rows).astype(jnp.int32)
        band_padded = lax.dynamic_slice_in_dim(padded, low_row, band_rows + 6, 0)
        band_cotangent = lax.dynamic_slice_in_dim(cotangent, low_row, band_rows, 0)
        band_mask = lax.dynamic_slice_in_dim(keep_mask, low_row, band_rows, 0)
        result, gradients = block_pass(band_padded, band_cotangent, band_mask, kernel, gain, w_in, w_out)
        return (tuple((first_sum + second_sum for first_sum, second_sum in zip(totals, gradients))), result)
    totals, results = lax.scan(one_band, initial, jnp.arange(LAT_BANDS, dtype=jnp.int32))
    return (results.reshape((LAT_BANDS * band_rows,) + results.shape[2:]), totals)

def reference(atmos_state, ocean_state, atmos_cotangent, ocean_cotangent, land_sea, fold_partner, ocean_pairs, ocean_counts, ocean_weights, atmos_pairs, atmos_counts, atmos_weights, flux_map, surface_map, flux_inject, surface_inject, atmos_kernel, atmos_gain, atmos_w_in, atmos_w_out, ocean_kernel, ocean_gain, ocean_w_in, ocean_w_out):
    wet_cells = land_sea.astype(jnp.float32)
    atmos_fields = make_blocks(atmos_state, flux_map, jnp.ones((ALAT, LON_CELLS), jnp.float32), ABLK)
    ocean_fields = make_blocks(ocean_state, surface_map, wet_cells, OBLK)
    to_ocean = remap(atmos_fields, ocean_pairs, ocean_counts, ocean_weights)
    to_atmos = remap(ocean_fields, atmos_pairs, atmos_counts, atmos_weights)
    ocean_input = inject(ocean_state, to_ocean, OBLK, flux_inject)
    atmos_input = inject(atmos_state, to_atmos, ABLK, surface_inject)
    atmos_wide = jnp.concatenate([atmos_input[:, -3:], atmos_input, atmos_input[:, :3]], axis=1)
    atmos_padded = jnp.pad(atmos_wide, ((3, 3), (0, 0), (0, 0)))
    ocean_wide = jnp.concatenate([ocean_input[:, -3:], ocean_input, ocean_input[:, :3]], axis=1)
    top_rows = jnp.stack([ocean_input[OLAT - 1], ocean_input[OLAT - 2], ocean_input[OLAT - 3]])
    fold_columns = jnp.take(fold_partner, (jnp.arange(-3, LON_CELLS + 3) % LON_CELLS).astype(jnp.int32))
    folded = jnp.take(top_rows, fold_columns, axis=1)
    ocean_padded = jnp.concatenate([jnp.zeros((3, LON_CELLS + 6, CO), jnp.bfloat16), ocean_wide, folded], axis=0)
    atmos_next, atmos_grads = run_grid(atmos_padded, atmos_cotangent, jnp.ones((ALAT, LON_CELLS, 1), jnp.float32), atmos_kernel, atmos_gain, atmos_w_in, atmos_w_out, AR)
    ocean_next, ocean_grads = run_grid(ocean_padded, ocean_cotangent, wet_cells[:, :, None], ocean_kernel, ocean_gain, ocean_w_in, ocean_w_out, OR)
    return (atmos_next, ocean_next, atmos_grads[0], atmos_grads[1], atmos_grads[2], atmos_grads[3], ocean_grads[0], ocean_grads[1], ocean_grads[2], ocean_grads[3])
```

```python
import jax
import jax.numpy as jnp
from jax import lax
from jax.sharding import PartitionSpec as P

NFIELD = 16
BCELLS = 128
PAIRS = 4
LANES = 128


epsilon = 1e-06


def extended(shard, sides, width):
    for axis, dim in sides:
        devices, length = (lax.axis_size(axis), shard.shape[dim])
        up = [(i, (i + 1) % devices) for i in range(devices)]
        down = [(j, i) for i, j in up]
        last = lax.slice_in_dim(shard, length - width, length, axis=dim)
        initial = lax.slice_in_dim(shard, 0, width, axis=dim)
        before = lax.ppermute(last, axis, up)
        after = lax.ppermute(initial, axis, down)
        shard = jnp.concatenate([before, shard, after], axis=dim)
    return shard


def contract_rows(left, right):
    return lax.dot_general(
        left, right, (((0,), (0,)), ((), ())), preferred_element_type=jnp.float32
    )


def block_pass(padded, cotangent, keep_mask, kernel, gain, w_in, w_out):
    row_count = padded.shape[0] - 6
    col_count = padded.shape[1] - 6
    channels = padded.shape[2]
    convolved = jnp.zeros((row_count, col_count, channels), jnp.float32)
    for offset in range(49):
        tap_row = offset // 7
        tap_col = offset % 7
        window = padded[tap_row : tap_row + row_count, tap_col : tap_col + col_count, :].astype(
            jnp.float32
        )
        convolved = convolved + window * kernel[offset].astype(jnp.float32)
    centre = convolved - jnp.mean(convolved, axis=-1, keepdims=True)
    inv_spread = lax.rsqrt(jnp.mean(centre * centre, axis=-1, keepdims=True) + epsilon)
    unit_part = centre * inv_spread
    gain_wide = gain.astype(jnp.float32)
    normed = (unit_part * gain_wide).astype(jnp.bfloat16).reshape(row_count * col_count, channels)
    pre_act = jnp.dot(normed, w_in, preferred_element_type=jnp.float32)
    hidden = jax.nn.gelu(pre_act).astype(jnp.bfloat16)
    update = jnp.dot(hidden, w_out, preferred_element_type=jnp.float32).reshape(
        row_count, col_count, channels
    )
    interior = padded[3 : 3 + row_count, 3 : 3 + col_count, :].astype(jnp.float32)
    result = ((interior + update) * keep_mask).astype(jnp.bfloat16)
    upstream = (
        (cotangent.astype(jnp.float32) * keep_mask)
        .astype(jnp.bfloat16)
        .reshape(row_count * col_count, channels)
    )
    grad_out = contract_rows(hidden, upstream)
    grad_hidden = lax.dot_general(
        upstream, w_out, (((1,), (1,)), ((), ())), preferred_element_type=jnp.float32
    )
    _, gelu_back = jax.vjp(jax.nn.gelu, pre_act)
    grad_pre = gelu_back(grad_hidden)[0].astype(jnp.bfloat16)
    grad_in = contract_rows(normed, grad_pre)
    grad_normed = lax.dot_general(
        grad_pre, w_in, (((1,), (1,)), ((), ())), preferred_element_type=jnp.float32
    )
    grad_normed = grad_normed.reshape(row_count, col_count, channels)
    grad_gain = jnp.sum(grad_normed * unit_part, axis=(0, 1))
    grad_unit = grad_normed * gain_wide
    grad_conv = inv_spread * (
        grad_unit
        - jnp.mean(grad_unit, axis=-1, keepdims=True)
        - unit_part * jnp.mean(grad_unit * unit_part, axis=-1, keepdims=True)
    )
    tap_sums = []
    for offset in range(49):
        tap_row = offset // 7
        tap_col = offset % 7
        window = padded[tap_row : tap_row + row_count, tap_col : tap_col + col_count, :].astype(
            jnp.float32
        )
        tap_sums.append(jnp.sum(grad_conv * window, axis=(0, 1)))
    grad_kernel = jnp.stack(tap_sums)
    return (result, (grad_kernel, grad_gain, grad_in, grad_out))


def make_blocks(source, projection, keep_cells):
    channels = source.shape[2]
    shaped = source.reshape(-1, BCELLS, channels)
    values = jnp.einsum("nkc,cf->nfk", shaped, projection, preferred_element_type=jnp.float32)
    return (values * keep_cells.reshape(-1, 1, BCELLS)).astype(jnp.bfloat16)


def fetch_remap(source_blocks, pair_ids, pair_counts, remap_weights):
    lon_count = lax.axis_size("lon")
    lat_index = lax.axis_index("lat")
    lon_index = lax.axis_index("lon")
    source_count = source_blocks.shape[0]
    target_count = pair_ids.shape[0]
    placed = source_blocks[None, None]
    nearby = extended(placed, (("lat", 0), ("lon", 1)), 1)
    nearby = nearby.reshape(9 * source_count, NFIELD, BCELLS)
    flat_ids = pair_ids.reshape(-1)
    owners = flat_ids // source_count
    local_ids = flat_ids % source_count
    band_step = owners // lon_count - lat_index + 1
    sector_step = (owners % lon_count - lon_index + 1) % lon_count
    positions = (band_step * 3 + sector_step) * source_count + local_ids
    picked = jnp.take(nearby, positions, axis=0).reshape(target_count, PAIRS, NFIELD, BCELLS)
    in_use = (jnp.arange(PAIRS)[None, :] < pair_counts).astype(jnp.bfloat16)
    picked = picked * in_use[:, :, None, None]
    remapped = jnp.einsum(
        "nkfc,nkcd->nfd",
        picked,
        remap_weights.reshape(target_count, PAIRS, BCELLS, BCELLS),
        preferred_element_type=jnp.float32,
    )
    return remapped.astype(jnp.bfloat16)


def inject(state, remapped, projection):
    added = jnp.einsum("nfk,fc->nkc", remapped, projection, preferred_element_type=jnp.float32)
    return (state.astype(jnp.float32) + added.reshape(state.shape)).astype(jnp.bfloat16)


def pad_tile(source):
    padded = extended(source, (("lat", 0), ("lon", 1)), 3)
    lat_index = lax.axis_index("lat")
    lat_count = lax.axis_size("lat")
    rim_rows = jnp.arange(padded.shape[0])
    outside = (rim_rows < 3) & (lat_index == 0) | (rim_rows >= padded.shape[0] - 3) & (
        lat_index == lat_count - 1
    )
    padded = jnp.where(outside[:, None, None], jnp.zeros_like(padded), padded)
    return padded


def blocks_of(array):
    rows = array.reshape(-1, array.shape[-1])
    return [rows[:, at : at + LANES] for at in range(0, rows.shape[1], LANES)]


def exchanges(order):
    steps = []
    for axis in order:
        span = 1
        while span < lax.axis_size(axis):
            steps.append((axis, span))
            span *= 2
    near = ("lon", 1)
    if near in steps:
        steps.remove(near)
        steps.insert(0, near)
    return steps


def sum_over_devices(arrays, order):
    pieces = [piece for array in arrays for piece in blocks_of(array)]
    length = sum(piece.shape[0] for piece in pieces)
    steps = exchanges(order)
    unit = 16 * 2 ** len(steps)
    spare = -length % unit
    if spare:
        pieces.append(jnp.zeros((spare, LANES), jnp.float32))
    share = jnp.concatenate(pieces, axis=0)
    for axis, span in steps:
        half = share.shape[0] // 2
        bit = (lax.axis_index(axis) // span) % 2
        swap = [(i, i ^ span) for i in range(lax.axis_size(axis))]
        sent = lax.dynamic_slice_in_dim(share, (1 - bit) * half, half, 0)
        kept = lax.dynamic_slice_in_dim(share, bit * half, half, 0)
        share = kept + lax.ppermute(sent, axis, swap)
    share = share.astype(jnp.bfloat16)
    for axis, span in reversed(steps):
        bit = (lax.axis_index(axis) // span) % 2
        swap = [(i, i ^ span) for i in range(lax.axis_size(axis))]
        other = lax.ppermute(share, axis, swap)
        low = jnp.where(bit == 0, share, other)
        high = jnp.where(bit == 0, other, share)
        share = jnp.concatenate([low, high], axis=0)
    results = []
    at = 0
    for array in arrays:
        columns = array.shape[-1]
        rows = array.size // columns
        parts = []
        for _ in range(columns // LANES):
            parts.append(share[at : at + rows].astype(jnp.float32))
            at += rows
        results.append(jnp.concatenate(parts, axis=1).reshape(array.shape))
    return results


def shards(
    atmos_state,
    ocean_state,
    atmos_cotangent,
    ocean_cotangent,
    land_sea,
    fold_partner,
    ocean_pairs,
    ocean_counts,
    ocean_weights,
    atmos_pairs,
    atmos_counts,
    atmos_weights,
    flux_map,
    surface_map,
    flux_inject,
    surface_inject,
    atmos_kernel,
    atmos_gain,
    atmos_w_in,
    atmos_w_out,
    ocean_kernel,
    ocean_gain,
    ocean_w_in,
    ocean_w_out,
):
    wet_cells = land_sea.astype(jnp.float32)
    col_count = atmos_state.shape[1]
    atmos_fields = make_blocks(atmos_state, flux_map, jnp.ones(atmos_state.shape[:2], jnp.float32))
    ocean_fields = make_blocks(ocean_state, surface_map, wet_cells)
    to_ocean = fetch_remap(atmos_fields, ocean_pairs, ocean_counts, ocean_weights)
    to_atmos = fetch_remap(ocean_fields, atmos_pairs, atmos_counts, atmos_weights)
    ocean_input = inject(ocean_state, to_ocean, flux_inject)
    atmos_input = inject(atmos_state, to_atmos, surface_inject)
    atmos_padded = pad_tile(atmos_input)
    ocean_padded = pad_tile(ocean_input)
    top_rows = jnp.stack([ocean_input[-1], ocean_input[-2], ocean_input[-3]])
    whole_rows = lax.all_gather(top_rows, "lon", axis=1, tiled=True)
    first_column = lax.axis_index("lon") * col_count
    columns = (first_column - 3 + jnp.arange(col_count + 6, dtype=jnp.int32)) % whole_rows.shape[1]
    folded = jnp.take(whole_rows, jnp.take(fold_partner, columns), axis=1)
    is_top = lax.axis_index("lat") == lax.axis_size("lat") - 1
    ocean_padded = jnp.where(
        is_top, jnp.concatenate([ocean_padded[:-3], folded], axis=0), ocean_padded
    )
    atmos_next, atmos_grads = block_pass(
        atmos_padded,
        atmos_cotangent,
        jnp.ones(atmos_state.shape[:2] + (1,), jnp.float32),
        atmos_kernel,
        atmos_gain,
        atmos_w_in,
        atmos_w_out,
    )
    ocean_next, ocean_grads = block_pass(
        ocean_padded,
        ocean_cotangent,
        wet_cells[:, :, None],
        ocean_kernel,
        ocean_gain,
        ocean_w_in,
        ocean_w_out,
    )
    ocean_sums = sum_over_devices(ocean_grads, ("lon", "lat"))
    (atmos_out_sum,) = sum_over_devices(atmos_grads[3:], ("lat", "lon"))
    atmos_sums = sum_over_devices(atmos_grads[:3], ("lon", "lat"))
    summed = (*atmos_sums, atmos_out_sum, *ocean_sums)
    return (
        atmos_next,
        ocean_next,
        summed[0],
        summed[1],
        summed[2],
        summed[3],
        summed[4],
        summed[5],
        summed[6],
        summed[7],
    )


def solution(mesh):
    return jax.shard_map(
        shards,
        mesh=mesh,
        in_specs=(
            P("lat", "lon", None),
            P("lat", "lon", None),
            P("lat", "lon", None),
            P("lat", "lon", None),
            P("lat", "lon"),
            P(),
            P("lat", "lon", None),
            P("lat", "lon"),
            P("lat", "lon", None, None, None),
            P("lat", "lon", None),
            P("lat", "lon"),
            P("lat", "lon", None, None, None),
            P(),
            P(),
            P(),
            P(),
            P(),
            P(),
            P(),
            P(),
            P(),
            P(),
            P(),
            P(),
        ),
        out_specs=(
            P("lat", "lon", None),
            P("lat", "lon", None),
            P(),
            P(),
            P(),
            P(),
            P(),
            P(),
            P(),
            P(),
        ),
        check_vma=False,
    )
```
